256 devices in a mesh: floor: 8 (over x, core), facade: 32 (over z, y).
Axes of the slice: x: 4, y: 4, z: 8, core: 2. Of those that a mesh axis runs over, the one named last changes fastest.
Arguments:
- interface_rhs: float32 [8, 32, 2, 256, 128], P('floor', 'facade'), may hold values from -40 to 40
- inverse_factor: float32 [8, 32, 1024, 1024], P('floor', 'facade')
- near_coupling: bfloat16 [8, 32, 1024, 1024], P('floor', 'facade'), may hold values from -0.09375 to 0.09375
- near_pattern: int32 [8, 32, 8, 8], P('floor', 'facade'), may hold values from 0 to 1, as said below
Outputs:
- multipliers: float32 [8, 32, 2, 256, 128], P('floor', 'facade')
- residual: float32 [8, 32, 2, 256, 128], P('floor', 'facade')
The draws below stay inside these ranges and needn't reach their ends.
Inputs may be any that keep to these rules, and one draw needn't show every extreme that they name: `near_pattern`: every diagonal block is set; each subdomain has from 8 to 32 blocks set, and in every draw some subdomain has exactly 32.
All inputs are finite; a program needn't handle non-finite values.
Results may differ from the reference program's by a relative error of at most 0.0022.
Values sent between devices are 32-bit elements; how exact they have to be, the bound alone decides.
A program may use at most 64 MiB of HBM per device.

```python
import math
import jax
import jax.numpy as jnp
from jax import lax

FACE = 256
CASES = 128
NB = 8
ITERS = 4
NI = 1024
BLK = 128
MAXB = 32
FLOORS = 8
COLUMNS = 32


def draw_interface_rhs(key, part):
    key_base, key_rows, key_cases = jax.random.split(key, 3)
    full_shape = (FLOORS, COLUMNS, 2, FACE, CASES)
    base_draw = jnp.clip(jax.random.normal(key_base, full_shape, jnp.float32), -5.0, 5.0)
    row_scale = jnp.exp(jax.random.uniform(key_rows, (FLOORS, COLUMNS, 2, FACE, 1), jnp.float32, 0.0, math.log(10.0))) / math.sqrt(10.0)
    case_scale = jnp.exp(jax.random.uniform(key_cases, (1, 1, 1, 1, CASES), jnp.float32, 0.0, math.log(10.0))) / math.sqrt(10.0)
    floor_pos = jnp.arange(FLOORS).reshape(FLOORS, 1, 1, 1, 1)
    column_pos = jnp.arange(COLUMNS).reshape(1, COLUMNS, 1, 1, 1)
    position = (floor_pos * COLUMNS + column_pos).astype(jnp.float32)
    growth = jnp.sqrt(1.0 + 2.0 * position / max(FLOORS * COLUMNS - 1, 1))
    return jnp.clip(base_draw * row_scale * case_scale * growth, -40.0, 40.0)


def draw_inverse_factor(key, part):
    key_diag, key_off = jax.random.split(key)
    full_shape = (FLOORS, COLUMNS, NI, NI)
    diagonal = jax.random.uniform(key_diag, (FLOORS, COLUMNS, NI, 1), jnp.float32, 1.0, 3.0)
    spread = jnp.clip(jax.random.normal(key_off, full_shape, jnp.float32), -5.0, 5.0) * 0.5 / math.sqrt(NI)
    row_index = jnp.arange(NI).reshape(NI, 1)
    col_index = jnp.arange(NI).reshape(1, NI)
    identity = (row_index == col_index).astype(jnp.float32)
    return spread * (1.0 - identity) + identity * diagonal


def draw_near_pattern(key, part):
    key_first, key_second, key_heavy, key_order = jax.random.split(key, 4)
    spare_blocks = MAXB - NB
    first_draw = jax.random.randint(key_first, (FLOORS, COLUMNS), 0, spare_blocks + 1)
    second_draw = jax.random.randint(key_second, (FLOORS, COLUMNS), 0, spare_blocks + 1)
    counts = NB + first_draw * second_draw // max(spare_blocks, 1)
    heavy_device = jax.random.randint(key_heavy, (), 0, FLOORS * COLUMNS)
    flat_index = jnp.arange(FLOORS * COLUMNS).reshape(FLOORS, COLUMNS)
    counts = jnp.where(flat_index == heavy_device, MAXB, counts)
    block_ids = jnp.arange(NB * NB)
    scores = jax.random.randint(key_order, (FLOORS, COLUMNS, NB * NB), 0, 1 << 20) * (NB * NB) + block_ids
    on_diagonal = block_ids // NB == block_ids % NB
    scores = jnp.where(on_diagonal, -1 - block_ids, scores)
    block_rank = jnp.argsort(jnp.argsort(scores, axis=-1), axis=-1)
    live_blocks = (block_rank < counts[:, :, None]).astype(jnp.int32)
    return live_blocks.reshape(FLOORS, COLUMNS, NB, NB)


def levels(stream_key, shape, cuts, smallest, top_value):
    level, own = 1.0, jax.random.fold_in(stream_key, 6)
    for axis_at, blocks in cuts:
        heights = jnp.exp(jax.random.uniform(jax.random.fold_in(own, axis_at), (blocks,), jnp.float32, smallest / len(cuts), top_value / len(cuts)))
        level = level * jnp.repeat(heights, shape[axis_at] // blocks).reshape([-1 if axis == axis_at else 1 for axis in range(len(shape))])
    return level


def bell_draw(stream_key, dims, width, reach, cuts=(), held_as=jnp.bfloat16):
    result = jax.random.normal(stream_key, dims, jnp.float32) * width
    if len(cuts) > 0:
        result = levels(stream_key, dims, cuts, -0.22, 0.18) * result
    return jnp.clip(result, min=-reach, max=reach).astype(held_as)


def setup_inputs(seed: int = 0) -> dict:
    key_list = jax.random.split(jax.random.key(seed), 5)
    return {
        "interface_rhs": draw_interface_rhs(jax.random.fold_in(key_list[4], 71), 0),
        "inverse_factor": draw_inverse_factor(jax.random.fold_in(key_list[4], 71), 0),
        "near_coupling": bell_draw(key_list[2], (FLOORS, COLUMNS, NI, NI), (MAXB * BLK) ** -0.5, 0.09375, ((0, 8), (1, 32))),
        "near_pattern": draw_near_pattern(jax.random.fold_in(key_list[4], 71), 0),
    }


finest = lax.Precision.HIGHEST


def to_trace(owned):
    upper = owned[:, :, 0]
    right_face = owned[:, :, 1]
    below = jnp.concatenate([jnp.zeros_like(upper[:1]), upper[:-1]], axis=0)
    beside = jnp.roll(right_face, 1, axis=1)
    return jnp.stack([-below, upper, -beside, right_face], axis=2)


def from_trace(image, top_keep):
    above = jnp.concatenate([image[1:, :, 0], jnp.zeros_like(image[:1, :, 0])], axis=0)
    beyond = jnp.roll(image[:, :, 2], -1, axis=1)
    upper = (image[:, :, 1] - above) * top_keep
    return jnp.stack([upper, image[:, :, 3] - beyond], axis=2)


def local_floor(operands):
    factor, coupling, pattern, trace_form = operands
    columns = trace_form.shape[0]
    flat = trace_form.reshape(columns, 4 * FACE, CASES)
    inner = jnp.einsum("cij,cjr->cir", factor, flat, precision=finest)
    outer = jnp.einsum("cji,cjr->cir", factor, inner, precision=finest)
    expanded = jnp.repeat(jnp.repeat(pattern, BLK, axis=1), BLK, axis=2)
    masked = coupling.astype(jnp.float32) * expanded.astype(jnp.float32)
    rounded = lax.optimization_barrier(flat.astype(jnp.bfloat16)).astype(jnp.float32)
    forward = jnp.einsum("cij,cjr->cir", masked, rounded, precision=finest)
    forward = lax.optimization_barrier(forward.astype(jnp.bfloat16)).astype(jnp.float32)
    backward = jnp.einsum("cji,cjr->cir", masked, forward, precision=finest)
    return (outer + backward).reshape(columns, 4, FACE, CASES)


def apply_full(owned, inverse_factor, near_coupling, near_pattern, top_keep):
    trace_form = to_trace(owned)
    image = lax.map(local_floor, (inverse_factor, near_coupling, near_pattern, trace_form))
    return from_trace(image, top_keep)


def inner_product(left_side, right_side):
    return jnp.sum(left_side * right_side, axis=(0, 1, 2, 3))


def reference(interface_rhs, inverse_factor, near_coupling, near_pattern):
    top_keep = (jnp.arange(FLOORS) < FLOORS - 1).astype(jnp.float32).reshape(FLOORS, 1, 1, 1)
    rhs = jnp.stack([interface_rhs[:, :, 0] * top_keep, interface_rhs[:, :, 1]], axis=2)
    multipliers = jnp.zeros_like(rhs)
    residual = rhs
    direction = rhs
    norm_now = inner_product(residual, residual)
    for sweep in range(ITERS):
        image = apply_full(direction, inverse_factor, near_coupling, near_pattern, top_keep)
        step_size = norm_now / inner_product(direction, image)
        multipliers = multipliers + step_size * direction
        residual = residual - step_size * image
        norm_next = inner_product(residual, residual)
        direction = residual + (norm_next / norm_now) * direction
        norm_now = norm_next
    return multipliers, residual
```

```python
import functools

import jax
import jax.numpy as jnp
from jax import lax
from jax.experimental import pallas as pl
from jax.experimental.pallas import tpu as pltpu
from jax.sharding import PartitionSpec as P

ITERS = 4
RING = 4
F32 = jnp.float32
BF16 = jnp.bfloat16


def halves(value):
    high = value.astype(BF16)
    low = (value - high.astype(F32)).astype(BF16)
    return high, low


def kernel(
    floors,
    facades,
    rhs_hbm,
    w_hbm,
    near_hbm,
    pattern,
    x_ref,
    r_ref,
    w_land,
    near_land,
    w_hi,
    w_lo,
    wt_hi,
    wt_lo,
    near,
    near_t,
    a_hi,
    a_lo,
    uu,
    yy,
    recv,
    ww,
    zz,
    pp,
    ss,
    sums_out,
    sums_y,
    sums_f,
    sums_z,
    load_sem,
    face_send,
    face_recv,
    sum_send,
    sum_recv,
):
    size = w_land.shape[0]
    face = size // 4
    blocks = pattern.shape[2]
    blk = size // blocks
    f = lax.axis_index("floor")
    c = lax.axis_index("facade")
    ring = RING
    stack = facades // ring
    ypos = lax.rem(c, ring)
    zpos = lax.div(c, ring)
    keep = {0: (f > 0).astype(F32), 1: (f < floors - 1).astype(F32)}

    up = (lax.rem(f + 1, floors), c)
    down = (lax.rem(f + floors - 1, floors), c)
    right = (f, lax.rem(c + 1, facades))
    left = (f, lax.rem(c + facades - 1, facades))
    y_peers = [(f, zpos * ring + lax.rem(ypos + d, ring)) for d in range(1, ring)]
    f_peers = [(lax.rem(f + d, floors), c) for d in range(1, floors)]
    z_peers = [(f, lax.rem(zpos + d, stack) * ring + ypos) for d in range(1, stack)]

    chunk = size // blocks
    loads = []
    for i in range(blocks):
        rows = pl.ds(i * chunk, chunk)
        loads.append(pltpu.make_async_copy(w_hbm.at[0, 0, rows], w_land.at[rows], load_sem.at[i]))
    near_load = pltpu.make_async_copy(near_hbm.at[0, 0], near_land, load_sem.at[blocks])
    rhs_load = pltpu.make_async_copy(rhs_hbm.at[0, 0], r_ref, load_sem.at[blocks + 1])
    rhs_load.start()
    for copy in loads:
        copy.start()
    near_load.start()

    barrier = pltpu.get_barrier_semaphore()
    greeted = y_peers + f_peers + z_peers + [left, right]
    for peer in greeted:
        pl.semaphore_signal(barrier, inc=1, device_id=peer, device_id_type=pl.DeviceIdType.MESH)
    pl.semaphore_wait(barrier, len(greeted))

    def face_copy(source, k, slot, peer):
        return pltpu.make_async_remote_copy(
            src_ref=source,
            dst_ref=recv.at[k, slot],
            send_sem=face_send.at[k, slot],
            recv_sem=face_recv.at[k, slot],
            device_id=peer,
            device_id_type=pl.DeviceIdType.MESH,
        )

    first = {
        2: face_copy(rhs_hbm.at[0, 0, 1], ITERS, 2, right),
        0: face_copy(rhs_hbm.at[0, 0, 0], ITERS, 0, up),
    }
    for slot in (2, 0):
        first[slot].start()

    def split_rows(i):
        rows = pl.ds(pl.multiple_of(i * chunk, chunk), chunk)
        high, low = halves(w_land[rows, :])
        w_hi[rows, :] = high
        w_lo[rows, :] = low
        wt_hi[:, rows] = high.T
        wt_lo[:, rows] = low.T

    for i in range(blocks):
        loads[i].wait()
        split_rows(i)
    near_load.wait()

    def mask_rows(i, _):
        rows = pl.ds(pl.multiple_of(i * blk, blk), blk)
        for j in range(blocks):
            columns = pl.ds(j * blk, blk)
            kept = near_land[rows, columns].astype(F32) * pattern[0, 0, i, j].astype(F32)
            kept = kept.astype(BF16)
            near[rows, columns] = kept
            near_t[columns, rows] = kept.T
        return 0

    lax.fori_loop(0, blocks, mask_rows, 0)

    def product(left_side, right_side):
        return jnp.dot(left_side, right_side, preferred_element_type=F32)

    for i in range(4):
        rows = pl.ds(i * face, face)
        for j in range(i, 4):
            columns = pl.ds(j * face, face)
            total = product(wt_hi[rows, :], w_hi[:, columns])
            total += product(wt_hi[rows, :], w_lo[:, columns])
            total += product(wt_lo[rows, :], w_hi[:, columns])
            total += product(near_t[rows, :], near[:, columns])
            high, low = halves(total)
            a_hi[rows, columns] = high
            a_lo[rows, columns] = low
            if j > i:
                a_hi[columns, rows] = high.T
                a_lo[columns, rows] = low.T

    def set_input(slot, value):
        rows = pl.ds(slot * face, face)
        ww[rows, :] = value
        high, low = halves(value)
        uu[rows, 0 : value.shape[1]] = high
        uu[rows, value.shape[1] :] = low

    rhs_load.wait()
    r_ref[0] = r_ref[0] * keep[1]
    set_input(1, r_ref[0])
    set_input(3, r_ref[1])
    for slot in (0, 2):
        first[slot].wait()
        got = -recv[ITERS, slot]
        set_input(slot, got * keep[0] if slot == 0 else got)
    x_ref[...] = jnp.zeros_like(x_ref)
    pp[...] = jnp.zeros_like(pp)
    ss[...] = jnp.zeros_like(ss)
    zz[...] = jnp.zeros_like(zz)

    def sum_copy(k, stage, target, mine, peer):
        return pltpu.make_async_remote_copy(
            src_ref=sums_out.at[k, stage],
            dst_ref=target.at[k, mine],
            send_sem=sum_send.at[k, stage],
            recv_sem=sum_recv.at[k, stage],
            device_id=peer,
            device_id_type=pl.DeviceIdType.MESH,
        )

    stages = [(sums_y, ypos, y_peers), (sums_f, f, f_peers), (sums_z, zpos, z_peers)]

    def sums_start(k, stage, value):
        target, mine, peers = stages[stage]
        sums_out[k, stage] = value
        target[k, mine] = value
        for peer in peers:
            sum_copy(k, stage, target, mine, peer).start()

    def sums_end(k, stage):
        target, mine, peers = stages[stage]
        arrived = target.at[k, pl.ds(0, len(peers))]
        pltpu.make_async_copy(arrived, arrived, sum_recv.at[k, stage]).wait()
        total = target[k, 0]
        for i in range(1, len(peers) + 1):
            total += target[k, i]
        return total

    def own_sums():
        gamma = jnp.zeros((1, x_ref.shape[2]), F32)
        delta = gamma
        for own, slot in ((0, 1), (1, 3)):
            value = r_ref[own]
            gamma += jnp.sum(value * value, axis=0, keepdims=True)
            delta += jnp.sum(value * ww[slot * face : (slot + 1) * face, :], axis=0, keepdims=True)
        return jnp.concatenate([gamma, delta, jnp.zeros((6, gamma.shape[1]), F32)], axis=0)

    def apply_rows(k, slot):
        rows = pl.ds(slot * face, face)
        wide = product(a_hi[rows, :], uu[...]) + product(a_lo[rows, :], uu[...])
        cases = x_ref.shape[2]
        yy[k, slot] = wide[:, :cases] + wide[:, cases:]

    def coefficients(total, last_gamma, last_alpha):
        gamma = total[0:1]
        delta = total[1:2]
        beta = gamma / last_gamma
        alpha = gamma / (delta - beta * gamma / last_alpha)
        return gamma, alpha, beta

    def step_own(own, alpha, beta, old_w):
        fresh_s = old_w + beta * ss[own]
        fresh_p = r_ref[own] + beta * pp[own]
        ss[own] = fresh_s
        pp[own] = fresh_p
        x_ref[own] = x_ref[own] + alpha * fresh_p
        r_ref[own] = r_ref[own] - alpha * fresh_s

    def iteration(k, carry):
        last_gamma, last_alpha = carry
        first_time = k == 0
        begin = jnp.where(first_time, 1.0, 0.0).astype(F32)
        sums_start(k, 0, own_sums())
        apply_rows(k, 2)
        face_copy(yy.at[k, 2], k, 3, left).start()
        apply_rows(k, 3)
        face_copy(yy.at[k, 3], k, 2, right).start()
        sums_start(k, 1, sums_end(k, 0))
        apply_rows(k, 0)
        face_copy(yy.at[k, 0], k, 1, down).start()
        apply_rows(k, 1)
        face_copy(yy.at[k, 1], k, 0, up).start()
        sums_start(k, 2, sums_end(k, 1))
        total = sums_end(k, 2)
        gamma, alpha, beta = coefficients(total, last_gamma, last_alpha)
        alpha_w = alpha * (1.0 - begin) - begin
        alpha_x = alpha * (1.0 - begin)
        for slot in (0, 1, 2, 3):
            rows = pl.ds(slot * face, face)
            pltpu.make_async_copy(recv.at[k, slot], recv.at[k, slot], face_recv.at[k, slot]).wait()
            image = yy[k, slot] - recv[k, slot]
            if slot in keep:
                image = image * keep[slot]
            fresh_z = image + beta * zz[rows, :]
            zz[rows, :] = fresh_z
            old_w = ww[rows, :]
            if slot % 2 == 1:
                step_own(slot // 2, alpha_x, beta, old_w)
            set_input(slot, (1.0 - begin) * old_w - alpha_w * fresh_z)
        next_gamma = jnp.where(first_time, jnp.full_like(gamma, jnp.inf), gamma)
        next_alpha = jnp.where(first_time, jnp.ones_like(alpha), alpha)
        return next_gamma, next_alpha

    ones = jnp.ones((1, x_ref.shape[2]), F32)
    carry = (ones * jnp.inf, ones)
    carry = lax.fori_loop(0, ITERS, iteration, carry)

    sums_start(ITERS, 0, own_sums())
    sums_start(ITERS, 1, sums_end(ITERS, 0))
    sums_start(ITERS, 2, sums_end(ITERS, 1))
    total = sums_end(ITERS, 2)
    gamma, alpha, beta = coefficients(total, *carry)
    for own, slot in ((0, 1), (1, 3)):
        step_own(own, alpha, beta, ww[slot * face : (slot + 1) * face, :])

    def drain(k, _):
        for slot in range(4):
            pltpu.make_async_copy(recv.at[k, slot], recv.at[k, slot], face_send.at[k, slot]).wait()
        return 0

    lax.fori_loop(0, ITERS, drain, 0)

    def drain_sums(k, _):
        for stage in range(3):
            target, mine, peers = stages[stage]
            sent = target.at[k, pl.ds(0, len(peers))]
            pltpu.make_async_copy(sent, sent, sum_send.at[k, stage]).wait()
        return 0

    lax.fori_loop(0, ITERS + 1, drain_sums, 0)


def solution(mesh):
    floors = mesh.shape["floor"]
    facades = mesh.shape["facade"]

    def local(interface_rhs, inverse_factor, near_coupling, near_pattern):
        face, cases = interface_rhs.shape[3:]
        size = 4 * face
        blocks = near_pattern.shape[2]
        own = (2, face, cases)
        square = (size, size)
        outs = pl.pallas_call(
            functools.partial(kernel, floors, facades),
            out_shape=(jax.ShapeDtypeStruct(own, F32), jax.ShapeDtypeStruct(own, F32)),
            in_specs=[
                pl.BlockSpec(memory_space=pl.ANY),
                pl.BlockSpec(memory_space=pl.ANY),
                pl.BlockSpec(memory_space=pl.ANY),
                pl.BlockSpec(memory_space=pltpu.SMEM),
            ],
            out_specs=(
                pl.BlockSpec(memory_space=pltpu.VMEM),
                pl.BlockSpec(memory_space=pltpu.VMEM),
            ),
            scratch_shapes=[
                pltpu.VMEM(square, F32),
                pltpu.VMEM(square, BF16),
                pltpu.VMEM(square, BF16),
                pltpu.VMEM(square, BF16),
                pltpu.VMEM(square, BF16),
                pltpu.VMEM(square, BF16),
                pltpu.VMEM(square, BF16),
                pltpu.VMEM(square, BF16),
                pltpu.VMEM(square, BF16),
                pltpu.VMEM(square, BF16),
                pltpu.VMEM((size, 2 * cases), BF16),
                pltpu.VMEM((ITERS, 4, face, cases), F32),
                pltpu.VMEM((ITERS + 1, 4, face, cases), F32),
                pltpu.VMEM((size, cases), F32),
                pltpu.VMEM((size, cases), F32),
                pltpu.VMEM(own, F32),
                pltpu.VMEM(own, F32),
                pltpu.VMEM((ITERS + 1, 3, 8, cases), F32),
                pltpu.VMEM((ITERS + 1, RING, 8, cases), F32),
                pltpu.VMEM((ITERS + 1, floors, 8, cases), F32),
                pltpu.VMEM((ITERS + 1, facades // RING, 8, cases), F32),
                pltpu.SemaphoreType.DMA((blocks + 2,)),
                pltpu.SemaphoreType.DMA((ITERS + 1, 4)),
                pltpu.SemaphoreType.DMA((ITERS + 1, 4)),
                pltpu.SemaphoreType.DMA((ITERS + 1, 3)),
                pltpu.SemaphoreType.DMA((ITERS + 1, 3)),
            ],
            compiler_params=pltpu.CompilerParams(
                collective_id=0, has_side_effects=True, vmem_limit_bytes=48 << 20
            ),
        )(interface_rhs, inverse_factor, near_coupling, near_pattern)
        return tuple(value[None, None] for value in outs)

    vector = P("floor", "facade", None, None, None)
    matrix = P("floor", "facade", None, None)
    return jax.shard_map(
        local,
        mesh=mesh,
        in_specs=(vector, matrix, matrix, matrix),
        out_specs=(vector, vector),
        check_vma=False,
    )
```

```python
import functools

import jax
import jax.numpy as jnp
from jax import lax
from jax.experimental import pallas as pl
from jax.experimental.pallas import tpu as pltpu
from jax.sharding import PartitionSpec as P

ITERS = 4
RING = 4
F32 = jnp.float32
BF16 = jnp.bfloat16
MESH = pl.DeviceIdType.MESH


def halves(value):
    high = value.astype(BF16)
    low = (value - high.astype(F32)).astype(BF16)
    return high, low


def product(left_side, right_side):
    return jnp.dot(left_side, right_side, preferred_element_type=F32)


def tile_sum(value):
    rows, columns = value.shape
    tall = jnp.sum(value.reshape(rows // 8, 8, columns), axis=0)
    total = tall[:, 0:128]
    for start in range(128, columns, 128):
        total += tall[:, start : start + 128]
    return total


def column_sum(left_side, right_side):
    return jnp.sum(left_side * right_side, axis=0, keepdims=True)


def hankel_solve(entries, given):
    count = len(given)
    lower = [[None] * count for _ in range(count)]
    pivots = []
    for j in range(count):
        pivot = entries[2 * j]
        for k in range(j):
            pivot = pivot - lower[j][k] * lower[j][k] * pivots[k]
        pivots.append(pivot)
        for i in range(j + 1, count):
            value = entries[i + j]
            for k in range(j):
                value = value - lower[i][k] * lower[j][k] * pivots[k]
            lower[i][j] = value / pivot
    middle = []
    for i in range(count):
        value = given[i]
        for k in range(i):
            value = value - lower[i][k] * middle[k]
        middle.append(value)
    answer = [None] * count
    for i in reversed(range(count)):
        value = middle[i] / pivots[i]
        for k in range(i + 1, count):
            value = value - lower[k][i] * answer[k]
        answer[i] = value
    return answer


def kernel(
    floors,
    facades,
    rhs_hbm,
    w_hbm,
    near_hbm,
    pattern,
    x_ref,
    r_ref,
    w_land,
    near_land,
    rhs_land,
    w_hi,
    w_lo,
    wt_hi,
    wt_lo,
    near,
    near_t,
    a_ref,
    uu,
    part,
    yy,
    recv,
    vv,
    sums_out,
    sums_plane,
    sums_z,
    load_sem,
    face_send,
    face_recv,
    sum_send,
    sum_recv,
):
    size = w_land.shape[0]
    face = size // 4
    cases = x_ref.shape[2]
    blocks = pattern.shape[2]
    blk = size // blocks
    half = 2 * face
    f = lax.axis_index("floor")
    c = lax.axis_index("facade")
    stack = facades // RING
    ypos = lax.rem(c, RING)
    zpos = lax.div(c, RING)
    keep = {0: (f > 0).astype(F32), 1: (f < floors - 1).astype(F32)}

    up = (lax.rem(f + 1, floors), c)
    down = (lax.rem(f + floors - 1, floors), c)
    right = (f, lax.rem(c + 1, facades))
    left = (f, lax.rem(c + facades - 1, facades))
    steps = [(i, j) for i in range(floors) for j in range(RING) if i or j]
    steps.sort(key=lambda s: -(min(s[0], floors - s[0]) / 2 + min(s[1], RING - s[1])))
    plane_peers = [
        (lax.rem(f + i, floors), zpos * RING + lax.rem(ypos + j, RING)) for i, j in steps
    ]
    far = sorted(range(1, stack), key=lambda d: -min(d, stack - d))
    z_peers = [(f, lax.rem(zpos + d, stack) * RING + ypos) for d in far]

    loads = []
    for i in range(blocks):
        rows = pl.ds(i * blk, blk)
        loads.append(pltpu.make_async_copy(w_hbm.at[0, 0, rows], w_land.at[rows], load_sem.at[i]))
    near_load = pltpu.make_async_copy(near_hbm.at[0, 0], near_land, load_sem.at[blocks])
    rhs_load = pltpu.make_async_copy(rhs_hbm.at[0, 0], rhs_land, load_sem.at[blocks + 1])
    rhs_load.start()
    for copy in loads:
        copy.start()
    near_load.start()

    barrier = pltpu.get_barrier_semaphore()
    greeted = plane_peers + z_peers + [left, right]
    for peer in greeted:
        pl.semaphore_signal(barrier, inc=1, device_id=peer, device_id_type=MESH)

    squares = jnp.zeros((8, 128), F32)
    for i in range(blocks):
        loads[i].wait()
        rows = pl.ds(i * blk, blk)
        value = w_land[rows, :]
        high, low = halves(value)
        w_hi[rows, :] = high
        w_lo[rows, :] = low
        wt_hi[:, rows] = high.T
        wt_lo[:, rows] = low.T
        squares += tile_sum(value * value)

    rhs_load.wait()
    pl.semaphore_wait(barrier, len(greeted))

    def face_copy(source, k, slot, peer):
        return pltpu.make_async_remote_copy(
            src_ref=source,
            dst_ref=recv.at[k, slot],
            send_sem=face_send.at[k, slot],
            recv_sem=face_recv.at[k, slot],
            device_id=peer,
            device_id_type=MESH,
        )

    first = {
        2: face_copy(rhs_land.at[1], ITERS, 2, right),
        0: face_copy(rhs_land.at[0], ITERS, 0, up),
    }
    for slot in (2, 0):
        first[slot].start()

    near_load.wait()

    def mask_rows(i, total):
        rows = pl.ds(pl.multiple_of(i * blk, blk), blk)
        for j in range(blocks):
            columns = pl.ds(j * blk, blk)
            kept = near_land[rows, columns].astype(F32) * pattern[0, 0, i, j].astype(F32)
            total += tile_sum(kept * kept)
            kept = kept.astype(BF16)
            near[rows, columns] = kept
            near_t[columns, rows] = kept.T
        return total

    squares = lax.fori_loop(0, blocks, mask_rows, squares)

    stages = [
        (sums_plane, f * RING + ypos, plane_peers),
        (sums_z, zpos, z_peers),
    ]

    def sums_start(turn, stage, value):
        target, mine, peers = stages[stage]
        sums_out[turn, stage] = value
        target[turn, mine] = value
        for peer in peers:
            pltpu.make_async_remote_copy(
                src_ref=sums_out.at[turn, stage],
                dst_ref=target.at[turn, mine],
                send_sem=sum_send.at[turn, stage],
                recv_sem=sum_recv.at[turn, stage],
                device_id=peer,
                device_id_type=MESH,
            ).start()

    def sums_end(turn, stage):
        target, _, peers = stages[stage]
        arrived = target.at[turn, pl.ds(0, len(peers))]
        pltpu.make_async_copy(arrived, arrived, sum_recv.at[turn, stage]).wait()
        terms = [target[turn, i] for i in range(len(peers) + 1)]
        while len(terms) > 1:
            terms = [a + b for a, b in zip(terms[0::2], terms[1::2])]
        return terms[0]

    sums_start(0, 0, squares)

    for i in range(4):
        rows = pl.ds(i * face, face)
        for j in range(i, 4):
            columns = pl.ds(j * face, face)
            total = product(wt_hi[rows, :], w_hi[:, columns])
            total += product(wt_hi[rows, :], w_lo[:, columns])
            total += product(wt_lo[rows, :], w_hi[:, columns])
            total += product(near_t[rows, :], near[:, columns])
            high, low = halves(total)
            a_ref[i, 0, :, columns] = high
            a_ref[i, 1, :, columns] = low
            if j > i:
                a_ref[j, 0, :, rows] = high.T
                a_ref[j, 1, :, rows] = low.T

    def set_input(k, slot, value):
        vv[k, slot] = value
        rows = pl.ds(slot * face, face)
        high, low = halves(value)
        uu[rows, 0:cases] = high
        uu[rows, cases : 2 * cases] = low

    def products_of(slots, columns):
        slot = slots[0]
        lines = a_ref[slot : slot + 2, :, :, columns].reshape(4 * face, half)
        wide = product(lines, uu[columns, :])
        wide = wide[:, 0:cases] + wide[:, cases : 2 * cases]
        wide = wide.reshape(2, 2, face, cases)
        return [wide[i, 0] + wide[i, 1] for i in range(2)]

    def first_half():
        for slots in ((2, 3), (0, 1)):
            for slot, value in zip(slots, products_of(slots, pl.ds(0, half))):
                part[slot] = value

    def second_half(k, slots):
        for slot, value in zip(slots, products_of(slots, pl.ds(half, half))):
            yy[k, slot] = part[slot] + value

    def own_sums(left_side, right_side):
        return column_sum(vv[left_side, 1], vv[right_side, 1]) + column_sum(
            vv[left_side, 3], vv[right_side, 3]
        )

    def image_of(k, slot):
        image = yy[k, slot] - recv[k, slot]
        return image * keep[slot] if slot in keep else image

    set_input(0, 1, rhs_land[0] * keep[1])
    set_input(0, 3, rhs_land[1])
    first[0].wait()
    set_input(0, 0, -recv[ITERS, 0] * keep[0])
    first_half()
    sums_start(0, 1, sums_end(0, 0))
    first[2].wait()
    set_input(0, 2, -recv[ITERS, 2])

    moments = []
    sends = {0: (1, down), 1: (0, up), 2: (3, left), 3: (2, right)}
    for k in range(ITERS - 1):
        for slots in ((2, 3), (0, 1)):
            second_half(k, slots)
            for slot in slots:
                target, peer = sends[slot]
                face_copy(yy.at[k, slot], k, target, peer).start()
        if k > 0:
            moments.append(own_sums(k - 1, k))
        moments.append(own_sums(k, k))
        if k == 0:
            total = sums_end(0, 1)
            count = float(floors * facades * size)
            shift = jnp.sum(jnp.sum(total, axis=0, keepdims=True), axis=1, keepdims=True)
            shift = jnp.broadcast_to(shift * (2.0 / count), (1, cases))
            scale = 1.0 / shift
        for slot in (0, 1, 2, 3):
            pltpu.make_async_copy(recv.at[k, slot], recv.at[k, slot], face_recv.at[k, slot]).wait()
            fresh = (image_of(k, slot) - shift * vv[k, slot]) * scale
            set_input(k + 1, slot, fresh)
            if slot == 1:
                first_half()

    last = ITERS - 1
    second_half(last, (2, 3))
    second_half(last, (0, 1))
    energy = column_sum(vv[last, 0], yy[last, 0])
    for slot in range(1, 4):
        energy += column_sum(vv[last, slot], yy[last, slot])
    moments.append(own_sums(last - 1, last))
    moments.append(own_sums(last, last))
    sums_start(1, 0, jnp.concatenate(moments + [energy], axis=0))
    for slot in (2, 0):
        target, peer = sends[slot]
        face_copy(yy.at[last, slot], last, target, peer).start()
    sums_start(1, 1, sums_end(1, 0))
    total = sums_end(1, 1)

    given = [total[i : i + 1] for i in range(2 * ITERS - 1)]
    entries = [given[i + 1] * shift + given[i] * shift for i in range(2 * ITERS - 2)]
    entries.append(total[2 * ITERS - 1 : 2 * ITERS])
    answer = hankel_solve(entries, given[:ITERS])
    weights = []
    for i in range(ITERS):
        weight = (1.0 if i == 0 else -answer[i - 1] * shift) - answer[i] * shift if i < last else (
            -answer[i - 1] * shift
        )
        weights.append(weight)
    for own, slot in ((1, 3), (0, 1)):
        pltpu.make_async_copy(
            recv.at[last, slot], recv.at[last, slot], face_recv.at[last, slot]
        ).wait()
        solved = answer[0] * vv[0, slot]
        left_over = weights[0] * vv[0, slot]
        for i in range(1, ITERS):
            solved += answer[i] * vv[i, slot]
            left_over += weights[i] * vv[i, slot]
        x_ref[own] = solved
        r_ref[own] = left_over - answer[last] * image_of(last, slot)

    for k in range(ITERS):
        for slot in sends if k < last else (1, 3):
            pltpu.make_async_copy(recv.at[k, slot], recv.at[k, slot], face_send.at[k, slot]).wait()
    for turn in range(2):
        for stage in range(2):
            target, _, peers = stages[stage]
            sent = target.at[turn, pl.ds(0, len(peers))]
            pltpu.make_async_copy(sent, sent, sum_send.at[turn, stage]).wait()


def solution(mesh):
    floors = mesh.shape["floor"]
    facades = mesh.shape["facade"]

    def local(interface_rhs, inverse_factor, near_coupling, near_pattern):
        face, cases = interface_rhs.shape[3:]
        size = 4 * face
        blocks = near_pattern.shape[2]
        own = (2, face, cases)
        square = (size, size)
        outs = pl.pallas_call(
            functools.partial(kernel, floors, facades),
            out_shape=(jax.ShapeDtypeStruct(own, F32), jax.ShapeDtypeStruct(own, F32)),
            in_specs=[
                pl.BlockSpec(memory_space=pltpu.HBM),
                pl.BlockSpec(memory_space=pltpu.HBM),
                pl.BlockSpec(memory_space=pltpu.HBM),
                pl.BlockSpec(memory_space=pltpu.SMEM),
            ],
            out_specs=(
                pl.BlockSpec(memory_space=pltpu.VMEM),
                pl.BlockSpec(memory_space=pltpu.VMEM),
            ),
            scratch_shapes=[
                pltpu.VMEM(square, F32),
                pltpu.VMEM(square, BF16),
                pltpu.VMEM(own, F32),
                pltpu.VMEM(square, BF16),
                pltpu.VMEM(square, BF16),
                pltpu.VMEM(square, BF16),
                pltpu.VMEM(square, BF16),
                pltpu.VMEM(square, BF16),
                pltpu.VMEM(square, BF16),
                pltpu.VMEM((4, 2, face, size), BF16),
                pltpu.VMEM((size, 2 * cases), BF16),
                pltpu.VMEM((4, face, cases), F32),
                pltpu.VMEM((ITERS, 4, face, cases), F32),
                pltpu.VMEM((ITERS + 1, 4, face, cases), F32),
                pltpu.VMEM((ITERS, 4, face, cases), F32),
                pltpu.VMEM((2, 2, 8, cases), F32),
                pltpu.VMEM((2, floors * RING, 8, cases), F32),
                pltpu.VMEM((2, facades // RING, 8, cases), F32),
                pltpu.SemaphoreType.DMA((blocks + 2,)),
                pltpu.SemaphoreType.DMA((ITERS + 1, 4)),
                pltpu.SemaphoreType.DMA((ITERS + 1, 4)),
                pltpu.SemaphoreType.DMA((2, 2)),
                pltpu.SemaphoreType.DMA((2, 2)),
            ],
            compiler_params=pltpu.CompilerParams(
                collective_id=0, has_side_effects=True, vmem_limit_bytes=60 << 20
            ),
        )(interface_rhs, inverse_factor, near_coupling, near_pattern)
        return tuple(value[None, None] for value in outs)

    vector = P("floor", "facade", None, None, None)
    matrix = P("floor", "facade", None, None)
    return jax.shard_map(
        local,
        mesh=mesh,
        in_specs=(vector, matrix, matrix, matrix),
        out_specs=(vector, vector),
        check_vma=False,
    )
```

```python
import functools

import jax
import jax.numpy as jnp
from jax import lax
from jax.experimental import pallas as pl
from jax.experimental.pallas import tpu as pltpu
from jax.sharding import PartitionSpec as P

ITERS = 4
RING = 4
F32 = jnp.float32
BF16 = jnp.bfloat16
MESH = pl.DeviceIdType.MESH


def halves(value):
    high = value.astype(BF16)
    low = (value - high.astype(F32)).astype(BF16)
    return high, low


def product(left_side, right_side):
    return jnp.dot(left_side, right_side, preferred_element_type=F32)


def tile_sum(value):
    rows, columns = value.shape
    tall = jnp.sum(value.reshape(rows // 8, 8, columns), axis=0)
    total = tall[:, 0:128]
    for start in range(128, columns, 128):
        total += tall[:, start : start + 128]
    return total


def column_sum(left_side, right_side):
    return jnp.sum(left_side * right_side, axis=0, keepdims=True)


def hankel_solve(entries, given):
    count = len(given)
    lower = [[None] * count for _ in range(count)]
    pivots = []
    for j in range(count):
        pivot = entries[2 * j]
        for k in range(j):
            pivot = pivot - lower[j][k] * lower[j][k] * pivots[k]
        pivots.append(pivot)
        for i in range(j + 1, count):
            value = entries[i + j]
            for k in range(j):
                value = value - lower[i][k] * lower[j][k] * pivots[k]
            lower[i][j] = value / pivot
    middle = []
    for i in range(count):
        value = given[i]
        for k in range(i):
            value = value - lower[i][k] * middle[k]
        middle.append(value)
    answer = [None] * count
    for i in reversed(range(count)):
        value = middle[i] / pivots[i]
        for k in range(i + 1, count):
            value = value - lower[k][i] * answer[k]
        answer[i] = value
    return answer


def kernel(
    floors,
    facades,
    rhs_hbm,
    w_hbm,
    near_hbm,
    pattern_hbm,
    x_ref,
    r_ref,
    w_land,
    near_land,
    rhs_land,
    pattern,
    w_hi,
    w_lo,
    wt_hi,
    wt_lo,
    near,
    near_t,
    a_ref,
    uu,
    part,
    yy,
    recv,
    vv,
    sums_out,
    sums_plane,
    sums_z,
    few_out,
    few_plane,
    few_z,
    load_sem,
    face_send,
    face_recv,
    sum_send,
    sum_recv,
):
    size = w_land.shape[0]
    face = size // 4
    cases = x_ref.shape[2]
    blocks = pattern.shape[0]
    blk = size // blocks
    half = 2 * face
    f = lax.axis_index("floor")
    c = lax.axis_index("facade")
    stack = facades // RING
    ypos = lax.rem(c, RING)
    zpos = lax.div(c, RING)
    keep = {0: (f > 0).astype(F32), 1: (f < floors - 1).astype(F32)}

    up = (lax.rem(f + 1, floors), c)
    down = (lax.rem(f + floors - 1, floors), c)
    right = (f, lax.rem(c + 1, facades))
    left = (f, lax.rem(c + facades - 1, facades))
    steps = [(i, j) for i in range(floors) for j in range(RING) if i or j]
    steps.sort(key=lambda s: -(min(s[0], floors - s[0]) / 2 + min(s[1], RING - s[1])))
    plane_peers = [
        (lax.rem(f + i, floors), zpos * RING + lax.rem(ypos + j, RING)) for i, j in steps
    ]
    far = sorted(range(1, stack), key=lambda d: -min(d, stack - d))
    z_peers = [(f, lax.rem(zpos + d, stack) * RING + ypos) for d in far]

    loads = []
    for i in range(blocks):
        rows = pl.ds(i * blk, blk)
        loads.append(pltpu.make_async_copy(w_hbm.at[0, 0, rows], w_land.at[rows], load_sem.at[i]))
    near_load = pltpu.make_async_copy(near_hbm.at[0, 0], near_land, load_sem.at[blocks])
    rhs_load = pltpu.make_async_copy(rhs_hbm.at[0, 0], rhs_land, load_sem.at[blocks + 1])
    pattern_load = pltpu.make_async_copy(pattern_hbm.at[0, 0], pattern, load_sem.at[blocks + 2])
    rhs_load.start()
    for copy in loads:
        copy.start()
    near_load.start()
    pattern_load.start()

    barrier = pltpu.get_barrier_semaphore()
    greeted = plane_peers + z_peers + [left, right]
    for peer in greeted:
        pl.semaphore_signal(barrier, inc=1, device_id=peer, device_id_type=MESH)

    squares = jnp.zeros((8, 128), F32)
    for i in range(blocks):
        loads[i].wait()
        rows = pl.ds(i * blk, blk)
        value = w_land[rows, :]
        high, low = halves(value)
        w_hi[rows, :] = high
        w_lo[rows, :] = low
        wt_hi[:, rows] = high.T
        wt_lo[:, rows] = low.T
        squares += tile_sum(value * value)

    rhs_load.wait()
    pl.semaphore_wait(barrier, len(greeted))

    def face_copy(source, k, slot, peer):
        return pltpu.make_async_remote_copy(
            src_ref=source,
            dst_ref=recv.at[k, slot],
            send_sem=face_send.at[k, slot],
            recv_sem=face_recv.at[k, slot],
            device_id=peer,
            device_id_type=MESH,
        )

    first = {
        2: face_copy(rhs_land.at[1], ITERS, 2, right),
        0: face_copy(rhs_land.at[0], ITERS, 0, up),
    }
    for slot in (2, 0):
        first[slot].start()

    near_load.wait()
    pattern_load.wait()

    def mask_rows(i, total):
        rows = pl.ds(pl.multiple_of(i * blk, blk), blk)
        for j in range(blocks):
            columns = pl.ds(j * blk, blk)
            kept = near_land[rows, columns].astype(F32) * pattern[i, j].astype(F32)
            total += tile_sum(kept * kept)
            kept = kept.astype(BF16)
            near[rows, columns] = kept
            near_t[columns, rows] = kept.T
        return total

    squares = lax.fori_loop(0, blocks, mask_rows, squares)

    mine = (f * RING + ypos, zpos)
    peers_of = (plane_peers, z_peers)

    def buffers(turn, stage):
        if turn == 2:
            return few_out.at[stage], (few_plane, few_z)[stage]
        return sums_out.at[turn, stage], (sums_plane, sums_z)[stage].at[turn]

    def sums_start(turn, stage, value):
        source, target = buffers(turn, stage)
        source[...] = value
        target[mine[stage]] = value
        for peer in peers_of[stage]:
            pltpu.make_async_remote_copy(
                src_ref=source,
                dst_ref=target.at[mine[stage]],
                send_sem=sum_send.at[turn, stage],
                recv_sem=sum_recv.at[turn, stage],
                device_id=peer,
                device_id_type=MESH,
            ).start()

    def sums_wait(turn, stage, semaphores):
        _, target = buffers(turn, stage)
        moved = target.at[pl.ds(0, len(peers_of[stage]))]
        pltpu.make_async_copy(moved, moved, semaphores.at[turn, stage]).wait()

    def sums_end(turn, stage):
        sums_wait(turn, stage, sum_recv)
        _, target = buffers(turn, stage)
        terms = [target[i] for i in range(len(peers_of[stage]) + 1)]
        while len(terms) > 1:
            terms = [a + b for a, b in zip(terms[0::2], terms[1::2])]
        return terms[0]

    sums_start(0, 0, squares)

    for i in range(4):
        rows = pl.ds(i * face, face)
        for j in range(i, 4):
            columns = pl.ds(j * face, face)
            total = product(wt_hi[rows, :], w_hi[:, columns])
            total += product(wt_hi[rows, :], w_lo[:, columns])
            total += product(wt_lo[rows, :], w_hi[:, columns])
            total += product(near_t[rows, :], near[:, columns])
            high, low = halves(total)
            a_ref[i, 0, :, columns] = high
            a_ref[i, 1, :, columns] = low
            if j > i:
                a_ref[j, 0, :, rows] = high.T
                a_ref[j, 1, :, rows] = low.T

    def set_input(k, slot, value):
        vv[k, slot] = value
        rows = pl.ds(slot * face, face)
        high, low = halves(value)
        uu[rows, 0:cases] = high
        uu[rows, cases : 2 * cases] = low

    def products_of(slots, columns):
        slot = slots[0]
        lines = a_ref[slot : slot + 2, :, :, columns].reshape(4 * face, half)
        wide = product(lines, uu[columns, :])
        wide = wide[:, 0:cases] + wide[:, cases : 2 * cases]
        wide = wide.reshape(2, 2, face, cases)
        return [wide[i, 0] + wide[i, 1] for i in range(2)]

    def first_half():
        for slots in ((2, 3), (0, 1)):
            for slot, value in zip(slots, products_of(slots, pl.ds(0, half))):
                part[slot] = value

    def second_half(k, slots):
        for slot, value in zip(slots, products_of(slots, pl.ds(half, half))):
            yy[k, slot] = part[slot] + value

    def own_sums(left_side, right_side):
        return column_sum(vv[left_side, 1], vv[right_side, 1]) + column_sum(
            vv[left_side, 3], vv[right_side, 3]
        )

    def image_of(k, slot):
        image = yy[k, slot] - recv[k, slot]
        return image * keep[slot] if slot in keep else image

    set_input(0, 1, rhs_land[0] * keep[1])
    set_input(0, 3, rhs_land[1])
    first[0].wait()
    set_input(0, 0, -recv[ITERS, 0] * keep[0])
    first_half()
    sums_start(0, 1, sums_end(0, 0))
    first[2].wait()
    set_input(0, 2, -recv[ITERS, 2])

    last = ITERS - 1
    moments = []
    sends = {0: (1, down), 1: (0, up), 2: (3, left), 3: (2, right)}
    for k in range(last):
        for slots in ((2, 3), (0, 1)):
            second_half(k, slots)
            for slot in slots:
                target, peer = sends[slot]
                face_copy(yy.at[k, slot], k, target, peer).start()
        if k > 0:
            moments.append(own_sums(k - 1, k))
        moments.append(own_sums(k, k))
        if k == last - 1:
            blank = [jnp.zeros_like(moments[0])] * (8 - len(moments))
            sums_start(1, 0, jnp.concatenate(moments + blank, axis=0))
        if k == 0:
            total = sums_end(0, 1)
            count = float(floors * facades * size)
            shift = jnp.sum(jnp.sum(total, axis=0, keepdims=True), axis=1, keepdims=True)
            shift = jnp.broadcast_to(shift * (2.0 / count), (1, cases))
            scale = 1.0 / shift
        for slot in (0, 1, 2, 3):
            pltpu.make_async_copy(recv.at[k, slot], recv.at[k, slot], face_recv.at[k, slot]).wait()
            fresh = (image_of(k, slot) - shift * vv[k, slot]) * scale
            set_input(k + 1, slot, fresh)
            if slot == 1:
                first_half()

    second_half(last, (2, 3))
    second_half(last, (0, 1))
    energy = column_sum(vv[last, 0], yy[last, 0])
    for slot in range(1, 4):
        energy += column_sum(vv[last, slot], yy[last, slot])
    late = [own_sums(last - 1, last), own_sums(last, last), energy, jnp.zeros_like(energy)]
    sums_start(2, 0, jnp.concatenate(late, axis=0))
    for slot in (2, 0):
        target, peer = sends[slot]
        face_copy(yy.at[last, slot], last, target, peer).start()
    sums_start(1, 1, sums_end(1, 0))
    sums_start(2, 1, sums_end(2, 0))
    early = sums_end(1, 1)
    final = sums_end(2, 1)

    given = [early[i : i + 1] for i in range(len(moments))] + [final[0:1], final[1:2]]
    entries = [given[i + 1] * shift + given[i] * shift for i in range(2 * ITERS - 2)]
    entries.append(final[2:3])
    answer = hankel_solve(entries, given[:ITERS])
    weights = []
    for i in range(ITERS):
        weight = (1.0 if i == 0 else -answer[i - 1] * shift) - answer[i] * shift if i < last else (
            -answer[i - 1] * shift
        )
        weights.append(weight)
    for own, slot in ((1, 3), (0, 1)):
        pltpu.make_async_copy(
            recv.at[last, slot], recv.at[last, slot], face_recv.at[last, slot]
        ).wait()
        solved = answer[0] * vv[0, slot]
        left_over = weights[0] * vv[0, slot]
        for i in range(1, ITERS):
            solved += answer[i] * vv[i, slot]
            left_over += weights[i] * vv[i, slot]
        x_ref[own] = solved
        r_ref[own] = left_over - answer[last] * image_of(last, slot)

    for k in range(ITERS):
        for slot in sends if k < last else (1, 3):
            pltpu.make_async_copy(recv.at[k, slot], recv.at[k, slot], face_send.at[k, slot]).wait()
    for turn in range(3):
        for stage in range(2):
            sums_wait(turn, stage, sum_send)


def solution(mesh):
    floors = mesh.shape["floor"]
    facades = mesh.shape["facade"]

    def local(*operands):
        interface_rhs, _, _, near_pattern = operands
        face, cases = interface_rhs.shape[3:]
        size = 4 * face
        blocks = near_pattern.shape[2]
        own = (2, face, cases)
        square = (size, size)
        outs = pl.pallas_call(
            functools.partial(kernel, floors, facades),
            out_shape=(jax.ShapeDtypeStruct(own, F32), jax.ShapeDtypeStruct(own, F32)),
            in_specs=[
                pl.BlockSpec(memory_space=pltpu.HBM),
                pl.BlockSpec(memory_space=pltpu.HBM),
                pl.BlockSpec(memory_space=pltpu.HBM),
                pl.BlockSpec(memory_space=pltpu.HBM),
            ],
            out_specs=(
                pl.BlockSpec(memory_space=pltpu.VMEM),
                pl.BlockSpec(memory_space=pltpu.VMEM),
            ),
            scratch_shapes=[
                pltpu.VMEM(square, F32),
                pltpu.VMEM(square, BF16),
                pltpu.VMEM(own, F32),
                pltpu.SMEM((blocks, blocks), jnp.int32),
                pltpu.VMEM(square, BF16),
                pltpu.VMEM(square, BF16),
                pltpu.VMEM(square, BF16),
                pltpu.VMEM(square, BF16),
                pltpu.VMEM(square, BF16),
                pltpu.VMEM(square, BF16),
                pltpu.VMEM((4, 2, face, size), BF16),
                pltpu.VMEM((size, 2 * cases), BF16),
                pltpu.VMEM((4, face, cases), F32),
                pltpu.VMEM((ITERS, 4, face, cases), F32),
                pltpu.VMEM((ITERS + 1, 4, face, cases), F32),
                pltpu.VMEM((ITERS, 4, face, cases), F32),
                pltpu.VMEM((2, 2, 8, cases), F32),
                pltpu.VMEM((2, floors * RING, 8, cases), F32),
                pltpu.VMEM((2, facades // RING, 8, cases), F32),
                pltpu.VMEM((2, 4, cases), F32),
                pltpu.VMEM((floors * RING, 4, cases), F32),
                pltpu.VMEM((facades // RING, 4, cases), F32),
                pltpu.SemaphoreType.DMA((blocks + 3,)),
                pltpu.SemaphoreType.DMA((ITERS + 1, 4)),
                pltpu.SemaphoreType.DMA((ITERS + 1, 4)),
                pltpu.SemaphoreType.DMA((3, 2)),
                pltpu.SemaphoreType.DMA((3, 2)),
            ],
            compiler_params=pltpu.CompilerParams(
                collective_id=0, has_side_effects=True, vmem_limit_bytes=48 << 20
            ),
        )(*(pltpu.with_memory_space_constraint(value, pltpu.HBM) for value in operands))
        return tuple(value[None, None] for value in outs)

    vector = P("floor", "facade", None, None, None)
    matrix = P("floor", "facade", None, None)
    return jax.shard_map(
        local,
        mesh=mesh,
        in_specs=(vector, matrix, matrix, matrix),
        out_specs=(vector, vector),
        check_vma=False,
    )
```

```python
import functools

import jax
import jax.numpy as jnp
from jax import lax
from jax.experimental import pallas as pl
from jax.experimental.pallas import tpu as pltpu
from jax.sharding import PartitionSpec as P

ITERS = 4
RING = 4
F32 = jnp.float32
BF16 = jnp.bfloat16
MESH = pl.DeviceIdType.MESH


def halves(value):
    high = value.astype(BF16)
    low = (value - high.astype(F32)).astype(BF16)
    return high, low


def product(left_side, right_side):
    return jnp.dot(left_side, right_side, preferred_element_type=F32)


def tile_sum(value):
    rows, columns = value.shape
    tall = jnp.sum(value.reshape(rows // 8, 8, columns), axis=0)
    total = tall[:, 0:128]
    for start in range(128, columns, 128):
        total += tall[:, start : start + 128]
    return total


def column_sum(left_side, right_side):
    return jnp.sum(left_side * right_side, axis=0, keepdims=True)


def hankel_solve(entries, given):
    count = len(given)
    lower = [[None] * count for _ in range(count)]
    pivots = []
    for j in range(count):
        pivot = entries[2 * j]
        for k in range(j):
            pivot = pivot - lower[j][k] * lower[j][k] * pivots[k]
        pivots.append(pivot)
        for i in range(j + 1, count):
            value = entries[i + j]
            for k in range(j):
                value = value - lower[i][k] * lower[j][k] * pivots[k]
            lower[i][j] = value / pivot
    middle = []
    for i in range(count):
        value = given[i]
        for k in range(i):
            value = value - lower[i][k] * middle[k]
        middle.append(value)
    answer = [None] * count
    for i in reversed(range(count)):
        value = middle[i] / pivots[i]
        for k in range(i + 1, count):
            value = value - lower[k][i] * answer[k]
        answer[i] = value
    return answer


def kernel(
    floors,
    facades,
    rhs_hbm,
    w_hbm,
    near_hbm,
    pattern_hbm,
    x_ref,
    r_ref,
    w_land,
    near_land,
    rhs_land,
    pattern,
    w_hi,
    w_lo,
    wt_hi,
    wt_lo,
    near,
    near_t,
    a_ref,
    uu,
    part,
    yy,
    recv,
    vv,
    sums_out,
    sums_plane,
    sums_z,
    few_out,
    few_plane,
    few_z,
    load_sem,
    face_send,
    face_recv,
    sum_send,
    sum_recv,
):
    size = w_land.shape[0]
    face = size // 4
    cases = x_ref.shape[2]
    blocks = pattern.shape[0]
    blk = size // blocks
    half = 2 * face
    f = lax.axis_index("floor")
    c = lax.axis_index("facade")
    stack = facades // RING
    ypos = lax.rem(c, RING)
    zpos = lax.div(c, RING)
    keep = {0: (f > 0).astype(F32), 1: (f < floors - 1).astype(F32)}

    up = (lax.rem(f + 1, floors), c)
    down = (lax.rem(f + floors - 1, floors), c)
    right = (f, lax.rem(c + 1, facades))
    left = (f, lax.rem(c + facades - 1, facades))
    steps = [(i, j) for i in range(floors) for j in range(RING) if i or j]
    steps.sort(key=lambda s: -(min(s[0], floors - s[0]) / 2 + min(s[1], RING - s[1])))
    plane_peers = [
        (lax.rem(f + i, floors), zpos * RING + lax.rem(ypos + j, RING)) for i, j in steps
    ]
    far = sorted(range(1, stack), key=lambda d: -min(d, stack - d))
    z_peers = [(f, lax.rem(zpos + d, stack) * RING + ypos) for d in far]

    loads = []
    for i in range(blocks):
        rows = pl.ds(i * blk, blk)
        loads.append(pltpu.make_async_copy(w_hbm.at[0, 0, rows], w_land.at[rows], load_sem.at[i]))
    near_load = pltpu.make_async_copy(near_hbm.at[0, 0], near_land, load_sem.at[blocks])
    rhs_load = pltpu.make_async_copy(rhs_hbm.at[0, 0], rhs_land, load_sem.at[blocks + 1])
    pattern_load = pltpu.make_async_copy(pattern_hbm.at[0, 0], pattern, load_sem.at[blocks + 2])
    rhs_load.start()
    for copy in loads:
        copy.start()
    near_load.start()
    pattern_load.start()

    barrier = pltpu.get_barrier_semaphore()
    greeted = plane_peers + z_peers + [left, right]
    for peer in greeted:
        pl.semaphore_signal(barrier, inc=1, device_id=peer, device_id_type=MESH)

    squares = jnp.zeros((8, 128), F32)
    for i in range(blocks):
        loads[i].wait()
        rows = pl.ds(i * blk, blk)
        value = w_land[rows, :]
        high, low = halves(value)
        w_hi[rows, :] = high
        w_lo[rows, :] = low
        wt_hi[:, rows] = high.T
        wt_lo[:, rows] = low.T
        squares += tile_sum(value * value)

    rhs_load.wait()
    pl.semaphore_wait(barrier, len(greeted))

    def face_copy(source, k, slot, peer):
        return pltpu.make_async_remote_copy(
            src_ref=source,
            dst_ref=recv.at[k, slot],
            send_sem=face_send.at[k, slot],
            recv_sem=face_recv.at[k, slot],
            device_id=peer,
            device_id_type=MESH,
        )

    first = {
        2: face_copy(rhs_land.at[1], ITERS, 2, right),
        0: face_copy(rhs_land.at[0], ITERS, 0, up),
    }
    for slot in (2, 0):
        first[slot].start()

    near_load.wait()
    pattern_load.wait()

    def mask_rows(i, total):
        rows = pl.ds(pl.multiple_of(i * blk, blk), blk)
        for j in range(blocks):
            columns = pl.ds(j * blk, blk)
            kept = near_land[rows, columns].astype(F32) * pattern[i, j].astype(F32)
            total += tile_sum(kept * kept)
            kept = kept.astype(BF16)
            near[rows, columns] = kept
            near_t[columns, rows] = kept.T
        return total

    squares = lax.fori_loop(0, blocks, mask_rows, squares)

    mine = (f * RING + ypos, zpos)
    peers_of = (plane_peers, z_peers)

    def buffers(turn, stage):
        if turn == 1:
            return sums_out.at[stage], (sums_plane, sums_z)[stage]
        return few_out.at[turn // 2, stage], (few_plane, few_z)[stage].at[turn // 2]

    def sums_start(turn, stage, value):
        source, target = buffers(turn, stage)
        source[...] = value
        target[mine[stage]] = value
        for peer in peers_of[stage]:
            pltpu.make_async_remote_copy(
                src_ref=source,
                dst_ref=target.at[mine[stage]],
                send_sem=sum_send.at[turn, stage],
                recv_sem=sum_recv.at[turn, stage],
                device_id=peer,
                device_id_type=MESH,
            ).start()

    def sums_wait(turn, stage, semaphores):
        _, target = buffers(turn, stage)
        moved = target.at[pl.ds(0, len(peers_of[stage]))]
        pltpu.make_async_copy(moved, moved, semaphores.at[turn, stage]).wait()

    def sums_end(turn, stage):
        sums_wait(turn, stage, sum_recv)
        _, target = buffers(turn, stage)
        terms = [target[i] for i in range(len(peers_of[stage]) + 1)]
        while len(terms) > 1:
            terms = [a + b for a, b in zip(terms[0::2], terms[1::2])]
        return terms[0]

    sums_start(0, 0, squares[0:4] + squares[4:8])

    for i in range(4):
        rows = pl.ds(i * face, face)
        for j in range(i, 4):
            columns = pl.ds(j * face, face)
            total = product(wt_hi[rows, :], w_hi[:, columns])
            total += product(wt_hi[rows, :], w_lo[:, columns])
            total += product(wt_lo[rows, :], w_hi[:, columns])
            total += product(near_t[rows, :], near[:, columns])
            high, low = halves(total)
            a_ref[i, 0, :, columns] = high
            a_ref[i, 1, :, columns] = low
            if j > i:
                a_ref[j, 0, :, rows] = high.T
                a_ref[j, 1, :, rows] = low.T

    def set_input(k, slot, value):
        vv[k, slot] = value
        rows = pl.ds(slot * face, face)
        high, low = halves(value)
        uu[rows, 0:cases] = high
        uu[rows, cases : 2 * cases] = low

    def products_of(slots, columns):
        slot = slots[0]
        lines = a_ref[slot : slot + 2, :, :, columns].reshape(4 * face, half)
        wide = product(lines, uu[columns, :])
        wide = wide[:, 0:cases] + wide[:, cases : 2 * cases]
        wide = wide.reshape(2, 2, face, cases)
        return [wide[i, 0] + wide[i, 1] for i in range(2)]

    def first_half():
        for slots in ((2, 3), (0, 1)):
            for slot, value in zip(slots, products_of(slots, pl.ds(0, half))):
                part[slot] = value

    def second_half(k, slots):
        for slot, value in zip(slots, products_of(slots, pl.ds(half, half))):
            yy[k, slot] = part[slot] + value

    def own_sums(left_side, right_side):
        return column_sum(vv[left_side, 1], vv[right_side, 1]) + column_sum(
            vv[left_side, 3], vv[right_side, 3]
        )

    def image_of(k, slot):
        image = yy[k, slot] - recv[k, slot]
        return image * keep[slot] if slot in keep else image

    set_input(0, 1, rhs_land[0] * keep[1])
    set_input(0, 3, rhs_land[1])
    first[0].wait()
    set_input(0, 0, -recv[ITERS, 0] * keep[0])
    first_half()
    sums_start(0, 1, sums_end(0, 0))
    first[2].wait()
    set_input(0, 2, -recv[ITERS, 2])

    last = ITERS - 1
    moments = []
    sends = {0: (1, down), 1: (0, up), 2: (3, left), 3: (2, right)}
    for k in range(last):
        for slots in ((2, 3), (0, 1)):
            second_half(k, slots)
            for slot in slots:
                target, peer = sends[slot]
                face_copy(yy.at[k, slot], k, target, peer).start()
        if k > 0:
            moments.append(own_sums(k - 1, k))
        moments.append(own_sums(k, k))
        if k == last - 1:
            blank = [jnp.zeros_like(moments[0])] * (8 - len(moments))
            sums_start(1, 0, jnp.concatenate(moments + blank, axis=0))
        if k == 0:
            total = sums_end(0, 1)
            count = float(floors * facades * size)
            shift = jnp.sum(jnp.sum(total, axis=0, keepdims=True), axis=1, keepdims=True)
            shift = jnp.broadcast_to(shift * (2.0 / count), (1, cases))
            scale = 1.0 / shift
        for slot in (0, 1, 2, 3):
            pltpu.make_async_copy(recv.at[k, slot], recv.at[k, slot], face_recv.at[k, slot]).wait()
            fresh = (image_of(k, slot) - shift * vv[k, slot]) * scale
            set_input(k + 1, slot, fresh)
            if slot == 1:
                first_half()

    second_half(last, (2, 3))
    second_half(last, (0, 1))
    energy = column_sum(vv[last, 0], yy[last, 0])
    for slot in range(1, 4):
        energy += column_sum(vv[last, slot], yy[last, slot])
    late = [own_sums(last - 1, last), own_sums(last, last), energy, jnp.zeros_like(energy)]
    sums_start(2, 0, jnp.concatenate(late, axis=0))
    for slot in (2, 0):
        target, peer = sends[slot]
        face_copy(yy.at[last, slot], last, target, peer).start()
    sums_start(1, 1, sums_end(1, 0))
    sums_start(2, 1, sums_end(2, 0))
    early = sums_end(1, 1)
    final = sums_end(2, 1)

    given = [early[i : i + 1] for i in range(len(moments))] + [final[0:1], final[1:2]]
    entries = [given[i + 1] * shift + given[i] * shift for i in range(2 * ITERS - 2)]
    entries.append(final[2:3])
    answer = hankel_solve(entries, given[:ITERS])
    weights = []
    for i in range(ITERS):
        weight = (1.0 if i == 0 else -answer[i - 1] * shift) - answer[i] * shift if i < last else (
            -answer[i - 1] * shift
        )
        weights.append(weight)
    for own, slot in ((1, 3), (0, 1)):
        pltpu.make_async_copy(
            recv.at[last, slot], recv.at[last, slot], face_recv.at[last, slot]
        ).wait()
        solved = answer[0] * vv[0, slot]
        left_over = weights[0] * vv[0, slot]
        for i in range(1, ITERS):
            solved += answer[i] * vv[i, slot]
            left_over += weights[i] * vv[i, slot]
        x_ref[own] = solved
        r_ref[own] = left_over - answer[last] * image_of(last, slot)

    for k in range(ITERS):
        for slot in sends if k < last else (1, 3):
            pltpu.make_async_copy(recv.at[k, slot], recv.at[k, slot], face_send.at[k, slot]).wait()
    for turn in range(3):
        for stage in range(2):
            sums_wait(turn, stage, sum_send)


def write_out(x_ref, r_ref, x_out, r_out, sems):
    copies = [
        pltpu.make_async_copy(x_ref, x_out.at[0, 0], sems.at[0]),
        pltpu.make_async_copy(r_ref, r_out.at[0, 0], sems.at[1]),
    ]
    for copy in copies:
        copy.start()
    for copy in copies:
        copy.wait()


def solution(mesh):
    floors = mesh.shape["floor"]
    facades = mesh.shape["facade"]

    def local(*operands):
        interface_rhs, _, _, near_pattern = operands
        face, cases = interface_rhs.shape[3:]
        size = 4 * face
        blocks = near_pattern.shape[2]
        own = (2, face, cases)
        square = (size, size)
        outs = pl.pallas_call(
            functools.partial(kernel, floors, facades),
            out_shape=(jax.ShapeDtypeStruct(own, F32), jax.ShapeDtypeStruct(own, F32)),
            in_specs=[
                pl.BlockSpec(memory_space=pltpu.HBM),
                pl.BlockSpec(memory_space=pltpu.HBM),
                pl.BlockSpec(memory_space=pltpu.HBM),
                pl.BlockSpec(memory_space=pltpu.HBM),
            ],
            out_specs=(
                pl.BlockSpec(memory_space=pltpu.VMEM),
                pl.BlockSpec(memory_space=pltpu.VMEM),
            ),
            scratch_shapes=[
                pltpu.VMEM(square, F32),
                pltpu.VMEM(square, BF16),
                pltpu.VMEM(own, F32),
                pltpu.SMEM((blocks, blocks), jnp.int32),
                pltpu.VMEM(square, BF16),
                pltpu.VMEM(square, BF16),
                pltpu.VMEM(square, BF16),
                pltpu.VMEM(square, BF16),
                pltpu.VMEM(square, BF16),
                pltpu.VMEM(square, BF16),
                pltpu.VMEM((4, 2, face, size), BF16),
                pltpu.VMEM((size, 2 * cases), BF16),
                pltpu.VMEM((4, face, cases), F32),
                pltpu.VMEM((ITERS, 4, face, cases), F32),
                pltpu.VMEM((ITERS + 1, 4, face, cases), F32),
                pltpu.VMEM((ITERS, 4, face, cases), F32),
                pltpu.VMEM((2, 8, cases), F32),
                pltpu.VMEM((floors * RING, 8, cases), F32),
                pltpu.VMEM((facades // RING, 8, cases), F32),
                pltpu.VMEM((2, 2, 4, cases), F32),
                pltpu.VMEM((2, floors * RING, 4, cases), F32),
                pltpu.VMEM((2, facades // RING, 4, cases), F32),
                pltpu.SemaphoreType.DMA((blocks + 3,)),
                pltpu.SemaphoreType.DMA((ITERS + 1, 4)),
                pltpu.SemaphoreType.DMA((ITERS + 1, 4)),
                pltpu.SemaphoreType.DMA((3, 2)),
                pltpu.SemaphoreType.DMA((3, 2)),
            ],
            compiler_params=pltpu.CompilerParams(
                collective_id=0, has_side_effects=True, vmem_limit_bytes=48 << 20
            ),
        )(*(pltpu.with_memory_space_constraint(value, pltpu.HBM) for value in operands))
        whole = jax.ShapeDtypeStruct((1, 1, *own), F32)
        return pl.pallas_call(
            write_out,
            out_shape=(whole, whole),
            in_specs=[pl.BlockSpec(memory_space=pltpu.VMEM)] * 2,
            out_specs=[pl.BlockSpec(memory_space=pltpu.HBM)] * 2,
            scratch_shapes=[pltpu.SemaphoreType.DMA((2,))],
            compiler_params=pltpu.CompilerParams(vmem_limit_bytes=1 << 20),
        )(*(pltpu.with_memory_space_constraint(value, pltpu.VMEM) for value in outs))

    vector = P("floor", "facade", None, None, None)
    matrix = P("floor", "facade", None, None)
    return jax.shard_map(
        local,
        mesh=mesh,
        in_specs=(vector, matrix, matrix, matrix),
        out_specs=(vector, vector),
        check_vma=False,
    )
```

```python
import functools

import jax
import jax.numpy as jnp
from jax import lax
from jax.experimental import pallas as pl
from jax.experimental.pallas import tpu as pltpu
from jax.sharding import PartitionSpec as P

ITERS = 4
RING = 4
F32 = jnp.float32
BF16 = jnp.bfloat16
MESH = pl.DeviceIdType.MESH


def halves(value):
    high = value.astype(BF16)
    low = (value - high.astype(F32)).astype(BF16)
    return high, low


def product(left_side, right_side):
    return jnp.dot(left_side, right_side, preferred_element_type=F32)


def tile_sum(value):
    rows, columns = value.shape
    tall = jnp.sum(value.reshape(rows // 8, 8, columns), axis=0)
    total = tall[:, 0:128]
    for start in range(128, columns, 128):
        total += tall[:, start : start + 128]
    return total


def column_sum(left_side, right_side):
    return jnp.sum(left_side * right_side, axis=0, keepdims=True)


def hankel_solve(entries, given):
    count = len(given)
    lower = [[None] * count for _ in range(count)]
    pivots = []
    for j in range(count):
        pivot = entries[2 * j]
        for k in range(j):
            pivot = pivot - lower[j][k] * lower[j][k] * pivots[k]
        pivots.append(pivot)
        for i in range(j + 1, count):
            value = entries[i + j]
            for k in range(j):
                value = value - lower[i][k] * lower[j][k] * pivots[k]
            lower[i][j] = value / pivot
    middle = []
    for i in range(count):
        value = given[i]
        for k in range(i):
            value = value - lower[i][k] * middle[k]
        middle.append(value)
    answer = [None] * count
    for i in reversed(range(count)):
        value = middle[i] / pivots[i]
        for k in range(i + 1, count):
            value = value - lower[k][i] * answer[k]
        answer[i] = value
    return answer


def kernel(
    floors,
    facades,
    rhs_hbm,
    w_hbm,
    near_hbm,
    pattern_hbm,
    x_ref,
    r_ref,
    w_land,
    near_land,
    rhs_land,
    pattern,
    w_hi,
    w_lo,
    wt_hi,
    wt_lo,
    near,
    near_t,
    a_ref,
    uu,
    part,
    yy,
    recv,
    vv,
    sums_out,
    sums_plane,
    sums_z,
    few_out,
    few_plane,
    few_z,
    load_sem,
    face_send,
    face_recv,
    sum_send,
    sum_recv,
):
    size = w_land.shape[0]
    face = size // 4
    cases = x_ref.shape[2]
    blocks = pattern.shape[0]
    blk = size // blocks
    half = 2 * face
    f = lax.axis_index("floor")
    c = lax.axis_index("facade")
    stack = facades // RING
    ypos = lax.rem(c, RING)
    zpos = lax.div(c, RING)
    keep = {0: (f > 0).astype(F32), 1: (f < floors - 1).astype(F32)}

    up = (lax.rem(f + 1, floors), c)
    down = (lax.rem(f + floors - 1, floors), c)
    right = (f, lax.rem(c + 1, facades))
    left = (f, lax.rem(c + facades - 1, facades))
    steps = [(i, j) for i in range(floors) for j in range(RING) if i or j]
    steps.sort(key=lambda s: -(min(s[0], floors - s[0]) / 2 + min(s[1], RING - s[1])))
    plane_peers = [
        (lax.rem(f + i, floors), zpos * RING + lax.rem(ypos + j, RING)) for i, j in steps
    ]
    far = sorted(range(1, stack), key=lambda d: -min(d, stack - d))
    z_peers = [(f, lax.rem(zpos + d, stack) * RING + ypos) for d in far]

    loads = []
    for i in range(blocks):
        rows = pl.ds(i * blk, blk)
        loads.append(pltpu.make_async_copy(w_hbm.at[0, 0, rows], w_land.at[rows], load_sem.at[i]))
    near_load = pltpu.make_async_copy(near_hbm.at[0, 0], near_land, load_sem.at[blocks])
    rhs_load = pltpu.make_async_copy(rhs_hbm.at[0, 0], rhs_land, load_sem.at[blocks + 1])
    pattern_load = pltpu.make_async_copy(pattern_hbm.at[0, 0], pattern, load_sem.at[blocks + 2])
    rhs_load.start()
    for copy in loads:
        copy.start()
    near_load.start()
    pattern_load.start()

    barrier = pltpu.get_barrier_semaphore()
    greeted = plane_peers + z_peers + [left, right]
    for peer in greeted:
        pl.semaphore_signal(barrier, inc=1, device_id=peer, device_id_type=MESH)

    squares = jnp.zeros((8, 128), F32)
    for i in range(blocks):
        loads[i].wait()
        rows = pl.ds(i * blk, blk)
        value = w_land[rows, :]
        high, low = halves(value)
        w_hi[rows, :] = high
        w_lo[rows, :] = low
        wt_hi[:, rows] = high.T
        wt_lo[:, rows] = low.T
        squares += tile_sum(value * value)

    rhs_load.wait()
    pl.semaphore_wait(barrier, len(greeted))

    def face_copy(source, k, slot, peer):
        return pltpu.make_async_remote_copy(
            src_ref=source,
            dst_ref=recv.at[k, slot],
            send_sem=face_send.at[k, slot],
            recv_sem=face_recv.at[k, slot],
            device_id=peer,
            device_id_type=MESH,
        )

    first = {
        2: face_copy(rhs_land.at[1], ITERS, 2, right),
        0: face_copy(rhs_land.at[0], ITERS, 0, up),
    }
    for slot in (2, 0):
        first[slot].start()

    near_load.wait()
    pattern_load.wait()

    def mask_rows(i, total):
        rows = pl.ds(pl.multiple_of(i * blk, blk), blk)
        for j in range(blocks):
            columns = pl.ds(j * blk, blk)
            kept = near_land[rows, columns].astype(F32) * pattern[i, j].astype(F32)
            total += tile_sum(kept * kept)
            kept = kept.astype(BF16)
            near[rows, columns] = kept
            near_t[columns, rows] = kept.T
        return total

    squares = lax.fori_loop(0, blocks, mask_rows, squares)

    mine = (f * RING + ypos, zpos)
    peers_of = (plane_peers, z_peers)

    def buffers(turn, stage):
        if turn == 1:
            return sums_out.at[stage], (sums_plane, sums_z)[stage]
        return few_out.at[turn // 2, stage], (few_plane, few_z)[stage].at[turn // 2]

    def sums_start(turn, stage, value):
        source, target = buffers(turn, stage)
        source[...] = value
        target[mine[stage]] = value
        for peer in peers_of[stage]:
            pltpu.make_async_remote_copy(
                src_ref=source,
                dst_ref=target.at[mine[stage]],
                send_sem=sum_send.at[turn, stage],
                recv_sem=sum_recv.at[turn, stage],
                device_id=peer,
                device_id_type=MESH,
            ).start()

    def sums_wait(turn, stage, semaphores):
        _, target = buffers(turn, stage)
        moved = target.at[pl.ds(0, len(peers_of[stage]))]
        pltpu.make_async_copy(moved, moved, semaphores.at[turn, stage]).wait()

    def sums_end(turn, stage):
        sums_wait(turn, stage, sum_recv)
        _, target = buffers(turn, stage)
        terms = [target[i] for i in range(len(peers_of[stage]) + 1)]
        while len(terms) > 1:
            terms = [a + b for a, b in zip(terms[0::2], terms[1::2])]
        return terms[0]

    sums_start(0, 0, squares[0:4] + squares[4:8])

    for i in range(4):
        rows = pl.ds(i * face, face)
        for j in range(i, 4):
            columns = pl.ds(j * face, face)
            total = product(wt_hi[rows, :], w_hi[:, columns])
            total += product(wt_hi[rows, :], w_lo[:, columns])
            total += product(wt_lo[rows, :], w_hi[:, columns])
            total += product(near_t[rows, :], near[:, columns])
            high, low = halves(total)
            a_ref[i, 0, :, columns] = high
            a_ref[i, 1, :, columns] = low
            if j > i:
                a_ref[j, 0, :, rows] = high.T
                a_ref[j, 1, :, rows] = low.T

    def set_input(k, slot, value):
        vv[k, slot] = value
        rows = pl.ds(slot * face, face)
        high, low = halves(value)
        uu[rows, 0:cases] = high
        uu[rows, cases : 2 * cases] = low

    def products_of(slots, columns):
        slot = slots[0]
        lines = a_ref[slot : slot + 2, :, :, columns].reshape(4 * face, half)
        wide = product(lines, uu[columns, :])
        wide = wide[:, 0:cases] + wide[:, cases : 2 * cases]
        wide = wide.reshape(2, 2, face, cases)
        return [wide[i, 0] + wide[i, 1] for i in range(2)]

    def first_half():
        for slots in ((2, 3), (0, 1)):
            for slot, value in zip(slots, products_of(slots, pl.ds(0, half))):
                part[slot] = value

    def second_half(k, slots):
        for slot, value in zip(slots, products_of(slots, pl.ds(half, half))):
            yy[k, slot] = part[slot] + value

    def own_sums(left_side, right_side):
        return column_sum(vv[left_side, 1], vv[right_side, 1]) + column_sum(
            vv[left_side, 3], vv[right_side, 3]
        )

    def image_of(k, slot):
        image = yy[k, slot] - recv[k, slot]
        return image * keep[slot] if slot in keep else image

    set_input(0, 1, rhs_land[0] * keep[1])
    set_input(0, 3, rhs_land[1])
    first[0].wait()
    set_input(0, 0, -recv[ITERS, 0] * keep[0])
    first_half()
    sums_start(0, 1, sums_end(0, 0))
    first[2].wait()
    set_input(0, 2, -recv[ITERS, 2])

    last = ITERS - 1
    moments = []
    sends = {0: (1, down), 1: (0, up), 2: (3, left), 3: (2, right)}
    for k in range(last):
        for slots in ((2, 3), (0, 1)):
            second_half(k, slots)
            for slot in slots:
                target, peer = sends[slot]
                face_copy(yy.at[k, slot], k, target, peer).start()
        if k > 0:
            moments.append(own_sums(k - 1, k))
        moments.append(own_sums(k, k))
        if k == last - 1:
            blank = [jnp.zeros_like(moments[0])] * (8 - len(moments))
            sums_start(1, 0, jnp.concatenate(moments + blank, axis=0))
        if k == 0:
            total = sums_end(0, 1)
            count = float(floors * facades * size)
            shift = jnp.sum(jnp.sum(total, axis=0, keepdims=True), axis=1, keepdims=True)
            shift = jnp.broadcast_to(shift * (2.0 / count), (1, cases))
            scale = 1.0 / shift
        for slot in (0, 1, 2, 3):
            pltpu.make_async_copy(recv.at[k, slot], recv.at[k, slot], face_recv.at[k, slot]).wait()
            fresh = (image_of(k, slot) - shift * vv[k, slot]) * scale
            set_input(k + 1, slot, fresh)
            if slot == 1:
                first_half()

    second_half(last, (2, 3))
    energy = column_sum(vv[last, 0], part[0]) + column_sum(vv[last, 1], part[1])
    for slot in (2, 3):
        energy += column_sum(vv[last, slot], part[slot] + yy[last, slot])
    late = [own_sums(last - 1, last), own_sums(last, last), energy, jnp.zeros_like(energy)]
    sums_start(2, 0, jnp.concatenate(late, axis=0))
    second_half(last, (0, 1))
    for slot in (2, 0):
        target, peer = sends[slot]
        face_copy(yy.at[last, slot], last, target, peer).start()
    sums_start(1, 1, sums_end(1, 0))
    sums_start(2, 1, sums_end(2, 0))
    early = sums_end(1, 1)
    final = sums_end(2, 1)

    given = [early[i : i + 1] for i in range(len(moments))] + [final[0:1], final[1:2]]
    entries = [given[i + 1] * shift + given[i] * shift for i in range(2 * ITERS - 2)]
    entries.append(final[2:3])
    answer = hankel_solve(entries, given[:ITERS])
    weights = []
    for i in range(ITERS):
        weight = (1.0 if i == 0 else -answer[i - 1] * shift) - answer[i] * shift if i < last else (
            -answer[i - 1] * shift
        )
        weights.append(weight)
    for own, slot in ((1, 3), (0, 1)):
        pltpu.make_async_copy(
            recv.at[last, slot], recv.at[last, slot], face_recv.at[last, slot]
        ).wait()
        solved = answer[0] * vv[0, slot]
        left_over = weights[0] * vv[0, slot]
        for i in range(1, ITERS):
            solved += answer[i] * vv[i, slot]
            left_over += weights[i] * vv[i, slot]
        x_ref[own] = solved
        r_ref[own] = left_over - answer[last] * image_of(last, slot)

    for k in range(ITERS):
        for slot in sends if k < last else (1, 3):
            pltpu.make_async_copy(recv.at[k, slot], recv.at[k, slot], face_send.at[k, slot]).wait()
    for turn in range(3):
        for stage in range(2):
            sums_wait(turn, stage, sum_send)


def write_out(x_ref, r_ref, x_out, r_out, sems):
    copies = [
        pltpu.make_async_copy(x_ref, x_out.at[0, 0], sems.at[0]),
        pltpu.make_async_copy(r_ref, r_out.at[0, 0], sems.at[1]),
    ]
    for copy in copies:
        copy.start()
    for copy in copies:
        copy.wait()


def solution(mesh):
    floors = mesh.shape["floor"]
    facades = mesh.shape["facade"]

    def local(*operands):
        interface_rhs, _, _, near_pattern = operands
        face, cases = interface_rhs.shape[3:]
        size = 4 * face
        blocks = near_pattern.shape[2]
        own = (2, face, cases)
        square = (size, size)
        outs = pl.pallas_call(
            functools.partial(kernel, floors, facades),
            out_shape=(jax.ShapeDtypeStruct(own, F32), jax.ShapeDtypeStruct(own, F32)),
            in_specs=[
                pl.BlockSpec(memory_space=pltpu.HBM),
                pl.BlockSpec(memory_space=pltpu.HBM),
                pl.BlockSpec(memory_space=pltpu.HBM),
                pl.BlockSpec(memory_space=pltpu.HBM),
            ],
            out_specs=(
                pl.BlockSpec(memory_space=pltpu.VMEM),
                pl.BlockSpec(memory_space=pltpu.VMEM),
            ),
            scratch_shapes=[
                pltpu.VMEM(square, F32),
                pltpu.VMEM(square, BF16),
                pltpu.VMEM(own, F32),
                pltpu.SMEM((blocks, blocks), jnp.int32),
                pltpu.VMEM(square, BF16),
                pltpu.VMEM(square, BF16),
                pltpu.VMEM(square, BF16),
                pltpu.VMEM(square, BF16),
                pltpu.VMEM(square, BF16),
                pltpu.VMEM(square, BF16),
                pltpu.VMEM((4, 2, face, size), BF16),
                pltpu.VMEM((size, 2 * cases), BF16),
                pltpu.VMEM((4, face, cases), F32),
                pltpu.VMEM((ITERS, 4, face, cases), F32),
                pltpu.VMEM((ITERS + 1, 4, face, cases), F32),
                pltpu.VMEM((ITERS, 4, face, cases), F32),
                pltpu.VMEM((2, 8, cases), F32),
                pltpu.VMEM((floors * RING, 8, cases), F32),
                pltpu.VMEM((facades // RING, 8, cases), F32),
                pltpu.VMEM((2, 2, 4, cases), F32),
                pltpu.VMEM((2, floors * RING, 4, cases), F32),
                pltpu.VMEM((2, facades // RING, 4, cases), F32),
                pltpu.SemaphoreType.DMA((blocks + 3,)),
                pltpu.SemaphoreType.DMA((ITERS + 1, 4)),
                pltpu.SemaphoreType.DMA((ITERS + 1, 4)),
                pltpu.SemaphoreType.DMA((3, 2)),
                pltpu.SemaphoreType.DMA((3, 2)),
            ],
            compiler_params=pltpu.CompilerParams(
                collective_id=0, has_side_effects=True, vmem_limit_bytes=48 << 20
            ),
        )(*(pltpu.with_memory_space_constraint(value, pltpu.HBM) for value in operands))
        whole = jax.ShapeDtypeStruct((1, 1, *own), F32)
        return pl.pallas_call(
            write_out,
            out_shape=(whole, whole),
            in_specs=[pl.BlockSpec(memory_space=pltpu.VMEM)] * 2,
            out_specs=[pl.BlockSpec(memory_space=pltpu.HBM)] * 2,
            scratch_shapes=[pltpu.SemaphoreType.DMA((2,))],
            compiler_params=pltpu.CompilerParams(vmem_limit_bytes=1 << 20),
        )(*(pltpu.with_memory_space_constraint(value, pltpu.VMEM) for value in outs))

    vector = P("floor", "facade", None, None, None)
    matrix = P("floor", "facade", None, None)
    return jax.shard_map(
        local,
        mesh=mesh,
        in_specs=(vector, matrix, matrix, matrix),
        out_specs=(vector, vector),
        check_vma=False,
    )
```
